512 devices in a mesh: gx: 16 (over z_lo, x, core), gy: 8 (over y), sa: 4 (over z_hi).
Axes of the slice: x: 4, y: 8, z: 8 (z_hi: 4, z_lo: 2; z = z_hi * 2 + z_lo), core: 2. Of those that a mesh axis runs over, the one named last changes fastest.
Arguments:
- field: float32 [2, 2048, 128, 1024], P(None, 'gx', 'sa', 'gy'), may hold values from -6 to 6
- mode_two: float32 [1024, 128], P('gy'), may hold values from -0.1875 to 0.1875
- species: float32 [128, 32], P('sa'), may hold values from -0.5 to 0.5
Outputs:
- gram: float32 [2048, 2048], P('gx')
The draws below stay inside these ranges and needn't reach their ends.
All inputs are finite; a program needn't handle non-finite values.
Results may differ from the reference program's by a relative error of at most 0.0001.
Values sent between devices are 32-bit elements; how exact they have to be, the bound alone decides.
No kernel may reach another device: no remote copies, remote signals or barrier semaphores. Data moves between devices by JAX's collectives and lax.ppermute only.
A program may use at most 64 MiB of HBM per device.

```python
import jax
import jax.numpy as jnp
from jax import lax

NT = 2
R2 = 128
R3 = 32
NX = 2048
NY = 1024
NS = 128


def steps_of(own_key, dims, pieces, least, high):
    gain = 1.0
    for dim, blocks in pieces:
        steps = jax.random.uniform(jax.random.fold_in(jax.random.fold_in(own_key, 6), dim), (blocks,), jnp.float32, least / len(pieces), high / len(pieces))
        gain = gain * jnp.repeat(jnp.exp(steps), dims[dim] // blocks).reshape((-1,) + (1,) * (len(dims) - 1 - dim))
    return gain


def gaussian(own_key, dims, deviation, bound, shards=(), dtype=jnp.bfloat16):
    entries = deviation * jax.random.normal(own_key, dims, jnp.float32)
    if shards:
        entries = entries * steps_of(own_key, dims, shards, -0.22, 0.18)
    return jnp.clip(entries, -bound, bound).astype(dtype)


def setup_inputs(seed: int = 0) -> dict:
    keys = jax.random.split(jax.random.key(seed), 4)
    return {
        "field": gaussian(keys[0], (NT, NX, NS, NY), 1.0, 6.0, ((1, 16), (2, 4), (3, 8)), jnp.float32),
        "mode_two": gaussian(keys[1], (NY, R2), NY ** -0.5, 0.1875, ((0, 8),), jnp.float32),
        "species": gaussian(keys[2], (NS, R3), NS ** -0.5, 0.5, ((0, 4),), jnp.float32),
    }


def reduce_step(slab, mode_two, species):
    proj = jnp.einsum('isj,jr->isr', slab, mode_two, precision=lax.Precision.HIGHEST)
    return jnp.einsum('isr,sq->iqr', proj, species, precision=lax.Precision.HIGHEST)


def reference(field, mode_two, species):
    total = jnp.zeros((NX, NX), jnp.float32)
    for step in range(NT):
        core = reduce_step(field[step], mode_two, species)
        total = total + jnp.einsum('iqr,kqr->ik', core, core, precision=lax.Precision.HIGHEST)
    return total * (1.0 / (NT * R2 * R3))
```

```python
import jax
import jax.numpy as jnp
from jax import lax
from jax.experimental import pallas as pl
from jax.experimental.pallas import tpu as pltpu
from jax.sharding import Mesh
from jax.sharding import PartitionSpec as P

NT = 2
R2 = 128
R3 = 32
GX = ("gx_0", "gx_1", "gx_2")
HIGH = lax.Precision.HIGH


def sent_to_all(x, axis):
    copies = jnp.broadcast_to(x, (lax.axis_size(axis), *x.shape))
    return lax.all_to_all(copies, axis, split_axis=0, concat_axis=0, tiled=True)


def chain(local, axis, way, hops):
    devices = lax.axis_size(axis)
    me = lax.axis_index(axis)
    ring = [(i, (i + way) % devices) for i in range(devices)]
    moving = None
    for hop in range(hops):
        value = local((me + way * (hops - hop)) % devices)
        if moving is not None:
            value = value + moving
        moving = lax.ppermute(value, axis, ring)
    return moving


def transposed_kernel(x_ref, out_ref):
    for block in range(x_ref.shape[1]):
        lines = x_ref[:, block].reshape(128, 128)
        out_ref[:, block * 128 : (block + 1) * 128] = lines.T


def on_device(field, mode_two, species):
    devices = lax.axis_size("gy")
    me = lax.axis_index("gy")
    rows = field.shape[1] // devices

    def local_of(step):
        def local(chunk):
            slab = lax.dynamic_slice(field, (step, chunk * rows, 0, 0), (1, rows, *field.shape[2:]))[0]
            return jnp.einsum("isj,jr->isr", slab, mode_two, precision=HIGH)
        return local

    sums = []
    for step in range(NT):
        local = local_of(step)
        far = devices // 2
        down = chain(local, "gy", -1, far if step % 2 == 0 else devices - 1 - far)
        up = chain(local, "gy", 1, far if step % 2 == 1 else devices - 1 - far)
        sums.append(local(me) + down + up)
    proj = jnp.stack(sums)
    part = jnp.einsum("tisr,sq->qtir", proj, species, precision=HIGH)
    z = lax.axis_size("sa")
    part = part.reshape(z, -1, *part.shape[1:])
    core = jnp.sum(lax.all_to_all(part, "sa", 0, 0, tiled=True), axis=0)
    across = sent_to_all(core, "gy")
    x = sent_to_all(core, ("gx_0", "gx_1"))
    x = sent_to_all(x, "gx_2")
    all_rows = x.swapaxes(0, 1).reshape(-1, *core.shape)
    tile = jnp.einsum("gqtwr,yqtvr->gwyv", all_rows, across, precision=HIGH)
    tile = tile.reshape(z, -1, field.shape[1])
    tile = jnp.sum(lax.all_to_all(tile, "sa", 0, 0, tiled=True), axis=0) * (1.0 / (NT * R2 * R3))
    whole = sent_to_all(tile, ("gy", "sa"))
    whole = whole.reshape(devices, -1, rows, field.shape[1])
    return pl.pallas_call(
        transposed_kernel,
        out_shape=jax.ShapeDtypeStruct((128, 2048), jnp.float32),
    )(whole)


def solution(mesh):
    finer = Mesh(
        mesh.devices.reshape(2, 4, 2, mesh.shape["gy"], mesh.shape["sa"]),
        ("gx_0", "gx_1", "gx_2", "gy", "sa"),
    )
    return jax.shard_map(
        on_device,
        mesh=finer,
        in_specs=(P(None, GX, "sa", "gy"), P("gy", None), P("sa", None)),
        out_specs=P(GX, None),
        check_vma=False,
    )
```

```python
import jax
import jax.numpy as jnp
from jax import lax
from jax.experimental import pallas as pl
from jax.experimental.layout import Layout, with_layout_constraint
from jax.experimental.pallas import tpu as pltpu
from jax.sharding import Mesh
from jax.sharding import PartitionSpec as P

NT = 2
R2 = 128
R3 = 32
GX = ("gx_0", "gx_1", "gx_2")
HIGH = lax.Precision.HIGH


def sent_to_all(x, axis):
    copies = jnp.broadcast_to(x, (lax.axis_size(axis), *x.shape))
    return lax.all_to_all(copies, axis, split_axis=0, concat_axis=0, tiled=True)


def shifted(x, axis, way):
    devices = lax.axis_size(axis)
    return lax.ppermute(x, axis, [(i, (i + way) % devices) for i in range(devices)])


def halves(x):
    high = x.astype(jnp.bfloat16)
    low = (x - high.astype(jnp.float32)).astype(jnp.bfloat16)
    return high, low


def chain(local, axis, way, count):
    moving = None
    for left in range(count, 0, -1):
        value = local(way * left)
        if moving is not None:
            value = value + moving
        moving = shifted(value, axis, way)
    return moving


def summed_rows(field, mode_two, axis):
    devices = lax.axis_size(axis)
    me = lax.axis_index(axis)
    rows = field.shape[1] // devices
    proj = jnp.einsum("tisj,jr->tisr", field, mode_two, precision=HIGH)
    proj = with_layout_constraint(proj, Layout((0, 1, 2, 3)))
    pieces = {
        (step, k): lax.dynamic_slice(proj, (step, (me + k) % devices * rows, 0, 0), (1, rows, *proj.shape[2:]))[0]
        for step in range(NT) for k in range(devices)
    }
    pieces = lax.optimization_barrier(pieces)
    sums = []
    for step in range(NT):
        def local(offset):
            return pieces[step, offset % devices]

        far = devices // 2
        down = chain(local, axis, -1, far if step == 0 else devices - 1 - far)
        up = chain(local, axis, 1, far if step == 1 else devices - 1 - far)
        sums.append(local(0) + down + up)
    return jnp.stack(sums)


def gathered_rows(core):
    near = shifted(core, "gx_0", 1)
    pair = jnp.stack([core, near])
    x = jnp.stack([pair, shifted(pair, "gx_1", -1), shifted(pair, "gx_1", 2), shifted(pair, "gx_1", 1)])
    return x, shifted(x, "gx_2", 1)


def places():
    core, x, z = (lax.axis_index(axis) for axis in ("gx_2", "gx_1", "gx_0"))
    spots = [
        ((z + dz) % 2 * 4 + (x + dx) % 4) * 2 + (core + dc) % 2
        for dc in range(2) for dx in range(4) for dz in range(2)
    ]
    return jnp.stack(spots).astype(jnp.int32)


def gram_kernel(spots_ref, own_ref, other_ref, across_ref, out_ref):
    cuts, rows, width = across_ref.shape[1:]
    weights = []
    for cut in range(cuts):
        high, low = halves(across_ref[:, cut].reshape(-1, width))
        highs, lows = jnp.concatenate([high, high], axis=1), jnp.concatenate([low, low], axis=1)
        weights.append(jnp.concatenate([highs, lows], axis=0))
    spot = 0
    for side_ref in (own_ref, other_ref):
        total = None
        for cut in range(cuts):
            left = side_ref[:, :, cut].reshape(-1, width)
            doubled = jnp.concatenate(halves(left), axis=1)
            out = lax.dot_general(
                doubled, weights[cut], (((1,), (1,)), ((), ())), preferred_element_type=jnp.float32
            )
            total = out if total is None else total + out
        half = total.shape[1] // 2
        total = total[:, :half] + total[:, half:]
        for block in range(total.shape[0] // rows):
            place = pl.multiple_of(spots_ref[spot] * rows, rows)
            out_ref[pl.ds(place, rows), :] = total[block * rows : (block + 1) * rows]
            spot += 1


def tile_of(own, other, across):
    rows, width = across.shape[0] * across.shape[2], 2 * own.shape[0] * own.shape[1] * own.shape[3]
    whole = pl.BlockSpec(memory_space=pltpu.VMEM)
    return pl.pallas_call(
        gram_kernel,
        in_specs=[pl.BlockSpec(memory_space=pltpu.SMEM), whole, whole, whole],
        out_specs=whole,
        out_shape=jax.ShapeDtypeStruct((width, rows), jnp.float32),
        cost_estimate=pl.CostEstimate(flops=2**31, bytes_accessed=2**22, transcendentals=0),
    )(places(), own, other, across)


def transposed_kernel(x_ref, out_ref):
    for block in range(x_ref.shape[1]):
        lines = x_ref[:, block].reshape(-1, x_ref.shape[-1])
        out_ref[:, block * lines.shape[0] : (block + 1) * lines.shape[0]] = lines.T


def on_device(field, mode_two, species):
    devices = lax.axis_size("gy")
    proj = summed_rows(field, mode_two, "gy")
    part = jnp.einsum("tisr,sq->qtir", proj, species, precision=HIGH)
    z = lax.axis_size("sa")
    rows = part.shape[2]
    part = part.reshape(z, -1, rows, part.shape[-1])
    core = jnp.sum(lax.all_to_all(part, "sa", 0, 0, tiled=True), axis=0)
    across = sent_to_all(core, "gy")
    tile = tile_of(*gathered_rows(core), across)
    tile = lax.all_to_all(tile.reshape(z, -1, devices * rows), "sa", 0, 0, tiled=True)
    tile = jnp.sum(tile, axis=0) * (1.0 / (NT * R2 * R3))
    whole = sent_to_all(tile, ("gy", "sa"))
    whole = whole.reshape(devices, -1, rows, devices * rows)
    return pl.pallas_call(
        transposed_kernel,
        out_shape=jax.ShapeDtypeStruct((devices * rows, whole.shape[1] * devices * rows), jnp.float32),
    )(whole)


def solution(mesh):
    finer = Mesh(
        mesh.devices.reshape(2, 4, 2, mesh.shape["gy"], mesh.shape["sa"]),
        ("gx_0", "gx_1", "gx_2", "gy", "sa"),
    )
    return jax.shard_map(
        on_device,
        mesh=finer,
        in_specs=(P(None, GX, "sa", "gy"), P("gy", None), P("sa", None)),
        out_specs=P(GX, None),
        check_vma=False,
    )
```

```python
import jax
import jax.numpy as jnp
from jax import lax
from jax.experimental import pallas as pl
from jax.experimental.layout import Layout, with_layout_constraint
from jax.experimental.pallas import tpu as pltpu
from jax.sharding import Mesh
from jax.sharding import PartitionSpec as P


NT = 2
R2 = 128
R3 = 32
GX = ("gx_0", "gx_1", "gx_2")
HIGH = lax.Precision.HIGH


def sent_to_all(x, axis):
    copies = jnp.broadcast_to(x, (lax.axis_size(axis), *x.shape))
    return lax.all_to_all(copies, axis, split_axis=0, concat_axis=0, tiled=True)


def shifted(x, axis, way):
    devices = lax.axis_size(axis)
    return lax.ppermute(x, axis, [(i, (i + way) % devices) for i in range(devices)])


def halves(x):
    high = x.astype(jnp.bfloat16)
    low = (x - high.astype(jnp.float32)).astype(jnp.bfloat16)
    return high, low


def chain(local, axis, way, count):
    moving = None
    for left in range(count, 0, -1):
        value = local(way * left)
        if moving is not None:
            value = value + moving
        moving = shifted(value, axis, way)
    return moving


def summed_rows(field, mode_two, axis):
    devices = lax.axis_size(axis)
    me = lax.axis_index(axis)
    rows = field.shape[1] // devices
    proj = jnp.einsum("tisj,jr->tisr", field, mode_two, precision=HIGH)
    proj = with_layout_constraint(proj, Layout((0, 1, 2, 3)))
    pieces = {
        (step, k): lax.dynamic_slice(proj, (step, (me + k) % devices * rows, 0, 0), (1, rows, *proj.shape[2:]))[0]
        for step in range(NT) for k in range(devices)
    }
    pieces = lax.optimization_barrier(pieces)
    sums = []
    for step in range(NT):
        def local(offset):
            return pieces[step, offset % devices]

        far = devices // 2
        down = chain(local, axis, -1, far if step == 0 else devices - 1 - far)
        up = chain(local, axis, 1, far if step == 1 else devices - 1 - far)
        sums.append(local(0) + down + up)
    return jnp.stack(sums)


def gathered_rows(core):
    near = shifted(core, "gx_0", 1)
    pair = jnp.stack([core, near])
    x = jnp.stack([pair, shifted(pair, "gx_1", -1), shifted(pair, "gx_1", 2), shifted(pair, "gx_1", 1)])
    return x, shifted(x, "gx_2", 1)


def places():
    core, x, z = (lax.axis_index(axis) for axis in ("gx_2", "gx_1", "gx_0"))
    spots = [
        ((z + dz) % 2 * 4 + (x + dx) % 4) * 2 + (core + dc) % 2
        for dc in range(2) for dx in range(4) for dz in range(2)
    ]
    return jnp.stack(spots).astype(jnp.int32)


def gram_kernel(spots_ref, own_hbm, other_hbm, across_hbm, out_ref, own_ref, other_ref, across_ref, sems):
    refs = ((across_hbm, across_ref), (own_hbm, own_ref), (other_hbm, other_ref))
    copies = [pltpu.make_async_copy(source, target, sems.at[n]) for n, (source, target) in enumerate(refs)]
    for copy in copies:
        copy.start()
    cuts, rows, width = across_ref.shape[1:]
    copies[0].wait()
    weights = []
    for cut in range(cuts):
        high, low = halves(across_ref[:, cut].reshape(-1, width))
        highs, lows = jnp.concatenate([high, high], axis=1), jnp.concatenate([low, low], axis=1)
        weights.append(jnp.concatenate([highs, lows], axis=0))
    copies[1].wait()
    copies[2].wait()
    total = None
    for cut in range(cuts):
        left = [side_ref[:, :, cut].reshape(-1, width) for side_ref in (own_ref, other_ref)]
        doubled = jnp.concatenate(halves(jnp.concatenate(left, axis=0)), axis=1)
        out = lax.dot_general(doubled, weights[cut], (((1,), (1,)), ((), ())), preferred_element_type=jnp.float32)
        total = out if total is None else total + out
    half = total.shape[1] // 2
    total = total[:, :half] + total[:, half:]
    for spot in range(total.shape[0] // rows):
        place = pl.multiple_of(spots_ref[spot] * rows, rows)
        out_ref[pl.ds(place, rows), :] = total[spot * rows : (spot + 1) * rows]


def tile_of(own, other, across):
    rows, width = across.shape[0] * across.shape[2], 2 * own.shape[0] * own.shape[1] * own.shape[3]
    anywhere = pl.BlockSpec(memory_space=pl.ANY)
    return pl.pallas_call(
        gram_kernel,
        in_specs=[pl.BlockSpec(memory_space=pltpu.SMEM), anywhere, anywhere, anywhere],
        out_specs=pl.BlockSpec(memory_space=pltpu.VMEM),
        out_shape=jax.ShapeDtypeStruct((width, rows), jnp.float32),
        scratch_shapes=[
            pltpu.VMEM(own.shape, jnp.float32),
            pltpu.VMEM(other.shape, jnp.float32),
            pltpu.VMEM(across.shape, jnp.float32),
            pltpu.SemaphoreType.DMA((3,)),
        ],
        compiler_params=pltpu.CompilerParams(vmem_limit_bytes=2**24),
        cost_estimate=pl.CostEstimate(flops=2**31, bytes_accessed=2**22, transcendentals=0),
    )(places(), own, other, across)


def transposed_kernel(x_hbm, out_hbm, x_ref, out_ref, in_sems, out_sems):
    blocks, width = x_ref.shape[0], x_ref.shape[-1]
    columns = [pl.ds(block * width, width) for block in range(blocks)]
    incoming = [pltpu.make_async_copy(x_hbm.at[:, b], x_ref.at[b], in_sems.at[b]) for b in range(blocks)]
    outgoing = [pltpu.make_async_copy(out_ref.at[:, c], out_hbm.at[:, c], out_sems.at[b]) for b, c in enumerate(columns)]
    for copy in incoming:
        copy.start()
    for block in range(blocks):
        incoming[block].wait()
        out_ref[:, columns[block]] = x_ref[block].reshape(-1, width).T
        outgoing[block].start()
    for copy in outgoing:
        copy.wait()


def laid_out(whole):
    devices, blocks, rows, width = whole.shape
    shape = (width, blocks * devices * rows)
    anywhere = pl.BlockSpec(memory_space=pl.ANY)
    return pl.pallas_call(
        transposed_kernel,
        in_specs=[anywhere],
        out_specs=anywhere,
        out_shape=jax.ShapeDtypeStruct(shape, jnp.float32),
        scratch_shapes=[
            pltpu.VMEM((blocks, devices, rows, width), jnp.float32),
            pltpu.VMEM(shape, jnp.float32),
            pltpu.SemaphoreType.DMA((blocks,)),
            pltpu.SemaphoreType.DMA((blocks,)),
        ],
        compiler_params=pltpu.CompilerParams(vmem_limit_bytes=2**24),
    )(whole)


def on_device(field, mode_two, species):
    devices = lax.axis_size("gy")
    proj = summed_rows(field, mode_two, "gy")
    part = jnp.einsum("tisr,sq->qtir", proj, species, precision=HIGH)
    z = lax.axis_size("sa")
    rows = part.shape[2]
    part = part.reshape(z, -1, rows, part.shape[-1])
    core = jnp.sum(lax.all_to_all(part, "sa", 0, 0, tiled=True), axis=0)
    across = sent_to_all(core, "gy")
    gathered = gathered_rows(core)
    tile = tile_of(*gathered, across)
    tile = lax.all_to_all(tile.reshape(z, -1, devices * rows), "sa", 0, 0, tiled=True)
    tile = jnp.sum(tile, axis=0) * (1.0 / (NT * R2 * R3))
    whole = sent_to_all(tile, ("gy", "sa"))
    whole = whole.reshape(devices, -1, rows, devices * rows)
    return laid_out(whole)


def solution(mesh):
    finer = Mesh(
        mesh.devices.reshape(2, 4, 2, mesh.shape["gy"], mesh.shape["sa"]),
        ("gx_0", "gx_1", "gx_2", "gy", "sa"),
    )
    return jax.shard_map(
        on_device,
        mesh=finer,
        in_specs=(P(None, GX, "sa", "gy"), P("gy", None), P("sa", None)),
        out_specs=P(GX, None),
        check_vma=False,
    )
```
